128 devices in a mesh: seq: 32 (over z, y, core), head: 4 (over x).
Axes of the slice: x: 4, y: 4, z: 4, core: 2. Of those that a mesh axis runs over, the one named last changes fastest.
Arguments:
- queries: bfloat16 [32768, 4096], P('seq', 'head'), may hold values from -6 to 6
- keys: bfloat16 [32768, 4096], P('seq', 'head'), may hold values from -6 to 6
- values: bfloat16 [32768, 4096], P('seq', 'head'), may hold values from -6 to 6
- cluster_ids: int32 [4, 32768], P('head', 'seq'), may hold values from 0 to 1023, as said below
- slots: int32 [4, 32768], P('head', 'seq'), may hold values from 0 to 2, as said below
- centroid_sums: float32 [4, 1024, 1024], P('head', 'seq'), may hold values from -48 to 48
- centroid_counts: float32 [4, 1024], P('head', 'seq'), may hold values from 8 to 64
- out_weight: bfloat16 [4096, 4096], P('head'), may hold values from -0.09375 to 0.09375
Outputs:
- mixed: bfloat16 [32768, 4096], P(('seq', 'head'))
- centroids: float32 [4, 1024, 1024], P('head', 'seq')
The draws below stay inside these ranges and needn't reach their ends.
Inputs may be any that keep to these rules, and one draw needn't show every extreme that they name: `cluster_ids`: blocks are the aligned runs of 1024 tokens of one head group. In every block no cluster holds more than 3 tokens, and some cluster holds exactly 3; the clusters k * 32 to (k + 1) * 32 - 1 together hold at most 48 tokens of a block, and exactly 48 for some k in every block. Within one block the tokens of one cluster have slots 0, 1, 2, ... in the order of their positions.
All inputs are finite; a program needn't handle non-finite values.
Results may differ from the reference program's by a relative error of at most 0.015.
Values may be sent and summed in bfloat16 or wider, within the bound.
A program may use at most 192 MiB of HBM per device.

```python
import math
import jax
import jax.numpy as jnp
from jax import lax

D = 4096
HEADS = 32
HD = 128
CLUSTERS = 1024
SLOTS = 3
TOK_DEV = 1024
GROUPS = 4
GW = 1024
TOKENS = 32768
CL_DEV = 32
N_SEQ = 32


def block_routing(key, owner_first, local_first):
    owners = TOKENS // TOK_DEV
    per_owner = CLUSTERS // owners
    mean_load = TOK_DEV // owners
    owner_bound = 3 * mean_load // 2
    pair_count = per_owner * SLOTS
    subkeys = jax.random.split(key, 5)
    shuffle = jax.random.permutation(subkeys[0], owners).astype(jnp.int32)
    shuffle = jnp.where(shuffle == owner_first, shuffle[0], shuffle)
    shuffle = shuffle.at[0].set(owner_first)
    shifted_load = jax.random.randint(subkeys[1], (owners // 2,), 0, owner_bound - mean_load + 1, dtype=jnp.int32)
    shifted_load = shifted_load.at[0].set(owner_bound - mean_load)
    owner_load = jnp.full((owners,), mean_load, jnp.int32)
    owner_load = owner_load.at[shuffle[0::2]].add(shifted_load)
    owner_load = owner_load.at[shuffle[1::2]].add(-shifted_load)
    hotness = jax.random.randint(subkeys[2], (owners, per_owner), 0, 8, dtype=jnp.int32)
    hotness = hotness.at[owner_first, local_first].set(100)
    slot_level = jnp.arange(SLOTS, dtype=jnp.int32)
    tiebreak = jax.vmap(lambda sub: jax.random.permutation(sub, pair_count))(jax.random.split(subkeys[3], owners)).astype(jnp.int32)
    priority = ((hotness[:, :, None] - 4 * slot_level[None, None, :]) * 8192).reshape(owners, pair_count) + tiebreak
    sorted_pairs = jnp.argsort(-priority, axis=1)
    standing = jnp.argsort(sorted_pairs, axis=1).astype(jnp.int32)
    chosen = (standing < owner_load[:, None]).astype(jnp.int32)
    flat_index = jnp.arange(owners * pair_count, dtype=jnp.int32)
    marked = chosen.reshape(-1) * (owners * pair_count) + flat_index
    unused, picked = lax.top_k(marked, TOK_DEV)
    picked = picked.astype(jnp.int32)
    cluster_of = picked // pair_count * per_owner + picked // SLOTS % per_owner
    arrangement = jax.random.permutation(subkeys[4], TOK_DEV)
    cluster_of = cluster_of[arrangement]
    positions = jnp.arange(TOK_DEV, dtype=jnp.int32)
    earlier = (cluster_of[None, :] == cluster_of[:, None]) & (positions[None, :] < positions[:, None])
    slot_of = jnp.sum(earlier.astype(jnp.int32), axis=1)
    return (cluster_of, slot_of)


def routing_table(key):
    owners = TOKENS // TOK_DEV
    per_owner = CLUSTERS // owners
    group_keys = jax.random.split(jax.random.fold_in(key, 7), GROUPS)

    def one_group(group_key):
        subkeys = jax.random.split(group_key, 3)
        owner_first = jax.random.randint(subkeys[0], (), 0, owners, dtype=jnp.int32)
        local_first = jax.random.randint(subkeys[1], (), 0, per_owner, dtype=jnp.int32)
        block_keys = jax.random.split(subkeys[2], owners)
        cluster_of, slot_of = jax.vmap(lambda sub: block_routing(sub, owner_first, local_first))(block_keys)
        return (cluster_of.reshape(-1), slot_of.reshape(-1), owner_first * per_owner + local_first)
    return jax.vmap(one_group)(group_keys)


def paired_rows(key, second):
    base_noise = jax.random.normal(jax.random.fold_in(key, 31 + second), (TOKENS, GROUPS * GW), jnp.float32)
    return jnp.clip(base_noise, -6.0, 6.0)


def draw_queries(key, part):
    return paired_rows(key, 0).astype(jnp.bfloat16)


def draw_keys(key, part):
    return paired_rows(key, 1).astype(jnp.bfloat16)


def draw_cluster_ids(key, part):
    return routing_table(key)[0]


def draw_slots(key, part):
    return routing_table(key)[1]


def shard_levels(stream_key, extent, cuts, low, top_value):
    def one(position, blocks):
        heights = jax.random.uniform(jax.random.fold_in(jax.random.fold_in(stream_key, 6), position), (blocks,), jnp.float32, low / len(cuts), top_value / len(cuts))
        return jnp.repeat(jnp.exp(heights), extent[position] // blocks).reshape((-1,) + (1,) * (len(extent) - position - 1))

    gain = one(*cuts[0])
    for cut in cuts[1:]:
        gain = gain * one(*cut)
    return gain


def gaussian(own_key, extent, deviation, reach, pieces=(), kind=jnp.bfloat16):
    level = shard_levels(own_key, extent, pieces, -0.22, 0.18) if pieces else 1.0
    drawn = jax.random.normal(own_key, extent, jnp.float32) * deviation * level
    return jnp.minimum(jnp.maximum(drawn, -reach), reach).astype(kind)


def setup_inputs(seed: int = 0) -> dict:
    streams_of = jax.random.split(jax.random.key(seed), 9)
    return {
        "queries": draw_queries(jax.random.fold_in(streams_of[8], 71), 0),
        "keys": draw_keys(jax.random.fold_in(streams_of[8], 71), 0),
        "values": gaussian(streams_of[2], (TOKENS, HEADS * HD), 1.0, 6.0, ((0, 32), (1, 4))),
        "cluster_ids": draw_cluster_ids(jax.random.fold_in(streams_of[8], 71), 0),
        "slots": draw_slots(jax.random.fold_in(streams_of[8], 71), 0),
        "centroid_sums": jnp.clip(jax.random.uniform(streams_of[5], (GROUPS, CLUSTERS, GW), jnp.float32, -48.0, 48.0) * shard_levels(streams_of[5], (GROUPS, CLUSTERS, GW), ((0, 4), (1, 32)), -0.4, 0.0), -48.0, 48.0),
        "centroid_counts": jnp.clip(jnp.exp(math.log(64.0) - 2.0794415 * jax.random.uniform(streams_of[6], (GROUPS, CLUSTERS), jnp.float32) ** shard_levels(streams_of[6], (GROUPS, CLUSTERS), ((0, 4), (1, 32)), -0.2, 0.2)), 8.0, 64.0),
        "out_weight": gaussian(streams_of[7], (HEADS * HD, D), (HEADS * HD) ** -0.5, 0.09375, ((0, 4),)),
    }


def attend_clusters(cluster_rows, present):
    clusters_here, slot_count, packed_width = cluster_rows.shape
    row_width = packed_width // 3
    head_count = row_width // HD
    query_part = cluster_rows[:, :, :row_width].reshape(clusters_here, slot_count, head_count, HD).astype(jnp.float32)
    key_part = cluster_rows[:, :, row_width:2 * row_width].reshape(clusters_here, slot_count, head_count, HD).astype(jnp.float32)
    value_part = cluster_rows[:, :, 2 * row_width:].reshape(clusters_here, slot_count, head_count, HD).astype(jnp.float32)
    scores = jnp.einsum("crhd,cshd->chrs", query_part, key_part) * (HD ** -0.5)
    slot_index = jnp.arange(slot_count, dtype=jnp.int32)
    allowed = (present[:, None, None, :] > 0) & (slot_index[None, None, None, :] <= slot_index[None, None, :, None])
    scores = jnp.where(allowed, scores, -1e30)
    row_max = jnp.max(scores, axis=-1, keepdims=True)
    shifted = jnp.exp(scores - row_max)
    weights = (shifted / jnp.sum(shifted, axis=-1, keepdims=True)).astype(jnp.bfloat16)
    attended = jnp.einsum("chrs,cshd->crhd", weights.astype(jnp.float32), value_part)
    return attended.astype(jnp.bfloat16).reshape(clusters_here, slot_count, row_width)


def reference(queries, keys, values, cluster_ids, slots, centroid_sums, centroid_counts, out_weight):
    capacity = N_SEQ * SLOTS
    source_ids = jnp.arange(TOKENS, dtype=jnp.int32) // TOK_DEV

    def one_group(running, group_index):
        start = (group_index * GW).astype(jnp.int32)
        group_keys = lax.dynamic_slice_in_dim(keys, start, GW, 1)
        packed = jnp.concatenate([lax.dynamic_slice_in_dim(queries, start, GW, 1), group_keys, lax.dynamic_slice_in_dim(values, start, GW, 1)], axis=1)
        cluster_of = cluster_ids[group_index]
        slot_of = slots[group_index]
        target = (cluster_of * capacity + source_ids * SLOTS + slot_of).astype(jnp.int32)
        cluster_rows = jnp.zeros((CLUSTERS * capacity, 3 * GW), jnp.bfloat16).at[target].set(packed)
        present = jnp.zeros((CLUSTERS * capacity,), jnp.float32).at[target].set(1.0)
        attended = lax.map(lambda pair: attend_clusters(pair[0], pair[1]), (cluster_rows.reshape(N_SEQ, CL_DEV, capacity, 3 * GW), present.reshape(N_SEQ, CL_DEV, capacity)))
        own_rows = attended.reshape(CLUSTERS * capacity, GW)[target]
        group_weight = lax.dynamic_slice_in_dim(out_weight, start, GW, 0)
        partial_value = jnp.dot(own_rows.astype(jnp.float32), group_weight.astype(jnp.float32), preferred_element_type=jnp.float32).astype(jnp.bfloat16)
        partial_value = lax.optimization_barrier(partial_value)
        running = running + partial_value.astype(jnp.float32)
        batch_sums = jax.ops.segment_sum(group_keys.astype(jnp.float32), cluster_of, num_segments=CLUSTERS)
        batch_counts = jax.ops.segment_sum(jnp.ones((TOKENS,), jnp.float32), cluster_of, num_segments=CLUSTERS)
        return running, (batch_sums, batch_counts)

    running, (batch_sums, batch_counts) = lax.scan(one_group, jnp.zeros((TOKENS, D), jnp.float32), jnp.arange(GROUPS, dtype=jnp.int32))
    mixed = running.astype(jnp.bfloat16)
    centroids = (0.6 * centroid_sums + 0.4 * batch_sums) / (0.6 * centroid_counts + 0.4 * batch_counts)[:, :, None]
    return mixed, centroids
```

```python
import jax
import jax.numpy as jnp
from jax import lax
from jax.experimental import pallas as pl
from jax.experimental.pallas import tpu as pltpu
from jax.sharding import PartitionSpec as P

HD = 128
SLOTS = 3
SEGMENT = 48
TILE = 128
PACK_ROWS = 192
OUT_COLS = 512
NEG = -1e30


def pack_kernel(position_ref, queries_ref, keys_ref, values_ref, packed_ref):
    width = queries_ref.shape[1]
    rows, tokens = packed_ref.shape[0], queries_ref.shape[0]
    first = pl.program_id(0) * rows
    row_of = first + lax.broadcasted_iota(jnp.int32, (rows, tokens), 0)
    pick = (row_of == position_ref[...]).astype(jnp.bfloat16)
    for index, ref in enumerate((queries_ref, keys_ref, values_ref)):
        packed_ref[:, index * width : (index + 1) * width] = jnp.dot(
            pick, ref[...], preferred_element_type=jnp.float32
        ).astype(jnp.bfloat16)


def pack(position, queries, keys, values, rows):
    tokens, width = queries.shape
    whole = pl.BlockSpec((tokens, width), lambda i: (0, 0))
    return pl.pallas_call(
        pack_kernel,
        grid=(rows // PACK_ROWS,),
        in_specs=[pl.BlockSpec((1, tokens), lambda i: (0, 0)), whole, whole, whole],
        out_specs=pl.BlockSpec((PACK_ROWS, 3 * width), lambda i: (i, 0)),
        out_shape=jax.ShapeDtypeStruct((rows, 3 * width), jnp.bfloat16),
    )(position.reshape(1, tokens), queries, keys, values)


def attend_kernel(
    row_target_ref,
    column_target_ref,
    cluster_ref,
    first_ref,
    rows_ref,
    sums_ref,
    counts_ref,
    returned_ref,
    centroids_ref,
    ordered_ref,
    attended_ref,
):
    rows, packed_width = rows_ref.shape
    width = packed_width // 3
    clusters = sums_ref.shape[0]
    tiles = rows // TILE

    belongs = lax.broadcasted_iota(jnp.int32, (clusters, rows), 0) == cluster_ref[...]
    batch_sums = jnp.dot(
        belongs.astype(jnp.bfloat16),
        rows_ref[:, width : 2 * width],
        preferred_element_type=jnp.float32,
    )
    batch_counts = jnp.sum(belongs.astype(jnp.float32), axis=1, keepdims=True)
    centroids_ref[...] = (0.6 * sums_ref[...] + 0.4 * batch_sums) / (
        0.6 * counts_ref[...] + 0.4 * batch_counts
    )

    ordered_ref[0:TILE, :] = jnp.zeros((TILE, packed_width), jnp.bfloat16)

    def order(step, carry):
        start = step * (2 * TILE)
        place = start + lax.broadcasted_iota(jnp.int32, (2 * TILE, rows), 0)
        pick = (place == row_target_ref[...]).astype(jnp.bfloat16)
        for part in range(3):
            ordered_ref[pl.ds(start + TILE, 2 * TILE), part * width : (part + 1) * width] = (
                jnp.dot(
                    pick,
                    rows_ref[:, part * width : (part + 1) * width],
                    preferred_element_type=jnp.float32,
                ).astype(jnp.bfloat16)
            )
        return carry

    lax.fori_loop(0, tiles // 2, order, 0)

    def attend(step, carry):
        start = step * TILE
        place = start + lax.broadcasted_iota(jnp.int32, (TILE, first_ref.shape[1]), 0)
        first = first_ref[...]
        low = jnp.max(jnp.where(first <= place, first, 0), axis=1, keepdims=True)
        query_place = start + lax.broadcasted_iota(jnp.int32, (TILE, 2 * TILE), 0)
        key_place = start - TILE + lax.broadcasted_iota(jnp.int32, (TILE, 2 * TILE), 1)
        seen = (key_place <= query_place) & (key_place >= low)
        for head in range(width // HD):
            column = head * HD
            query = ordered_ref[pl.ds(start + TILE, TILE), column : column + HD]
            key = ordered_ref[pl.ds(start, 2 * TILE), width + column : width + column + HD]
            value = ordered_ref[
                pl.ds(start, 2 * TILE), 2 * width + column : 2 * width + column + HD
            ]
            scores = lax.dot_general(
                query, key, (((1,), (1,)), ((), ())), preferred_element_type=jnp.float32
            ) * (HD**-0.5)
            scores = jnp.where(seen, scores, NEG)
            shifted = jnp.exp(scores - jnp.max(scores, axis=1, keepdims=True))
            weights = shifted / jnp.sum(shifted, axis=1, keepdims=True)
            attended_ref[pl.ds(start, TILE), column : column + HD] = jnp.dot(
                weights.astype(jnp.bfloat16), value, preferred_element_type=jnp.float32
            ).astype(jnp.bfloat16)
        return carry

    lax.fori_loop(0, tiles, attend, 0)

    def restore(step, carry):
        start = step * (2 * TILE)
        target = column_target_ref[pl.ds(start, 2 * TILE), :]
        pick = (lax.broadcasted_iota(jnp.int32, (2 * TILE, rows), 1) == target).astype(jnp.bfloat16)
        returned_ref[pl.ds(start, 2 * TILE), :] = jnp.dot(
            pick, attended_ref[...], preferred_element_type=jnp.float32
        ).astype(jnp.bfloat16)
        return carry

    lax.fori_loop(0, tiles // 2, restore, 0)


def attend_clusters(target, cluster, first, rows, sums, counts):
    total, packed_width = rows.shape
    width = packed_width // 3
    clusters = sums.shape[0]
    vmem = pl.BlockSpec(memory_space=pltpu.VMEM)
    return pl.pallas_call(
        attend_kernel,
        in_specs=[vmem] * 7,
        out_specs=[vmem] * 2,
        out_shape=[
            jax.ShapeDtypeStruct((total, width), jnp.bfloat16),
            jax.ShapeDtypeStruct((clusters, width), jnp.float32),
        ],
        scratch_shapes=[
            pltpu.VMEM((total + TILE, packed_width), jnp.bfloat16),
            pltpu.VMEM((total, width), jnp.bfloat16),
        ],
        compiler_params=pltpu.CompilerParams(vmem_limit_bytes=60 << 20),
    )(
        target.reshape(1, total),
        target.reshape(total, 1),
        cluster.reshape(1, total),
        first,
        rows,
        sums,
        counts,
    )


def project_kernel(position_ref, rows_ref, weight_ref, out_ref, own_ref):
    tokens, total = own_ref.shape[0], rows_ref.shape[0]

    @pl.when(pl.program_id(0) == 0)
    def _():
        pick = (lax.broadcasted_iota(jnp.int32, (tokens, total), 1) == position_ref[...]).astype(
            jnp.bfloat16
        )
        own_ref[...] = jnp.dot(pick, rows_ref[...], preferred_element_type=jnp.float32).astype(
            jnp.bfloat16
        )

    out_ref[...] = jnp.dot(
        own_ref[...], weight_ref[...], preferred_element_type=jnp.float32
    ).astype(jnp.bfloat16)


def project(position, rows, weight):
    tokens = position.shape[0]
    total, width = rows.shape
    columns = weight.shape[1]
    return pl.pallas_call(
        project_kernel,
        grid=(columns // OUT_COLS,),
        in_specs=[
            pl.BlockSpec((tokens, 1), lambda i: (0, 0)),
            pl.BlockSpec((total, width), lambda i: (0, 0)),
            pl.BlockSpec((width, OUT_COLS), lambda i: (0, i)),
        ],
        out_specs=pl.BlockSpec((tokens, OUT_COLS), lambda i: (0, i)),
        out_shape=jax.ShapeDtypeStruct((tokens, columns), jnp.bfloat16),
        scratch_shapes=[pltpu.VMEM((tokens, width), jnp.bfloat16)],
    )(position.reshape(tokens, 1), rows, weight)


def block_positions(cluster_of, owners, per_owner):
    tokens = cluster_of.shape[0]
    owner_of = cluster_of // per_owner
    belongs = (jnp.arange(owners, dtype=jnp.int32)[:, None] == owner_of[None, :]).astype(
        jnp.bfloat16
    )
    token = jnp.arange(tokens, dtype=jnp.int32)
    earlier = (token[:, None] < token[None, :]).astype(jnp.bfloat16)
    before = jnp.dot(belongs, earlier, preferred_element_type=jnp.float32)
    rank = jnp.sum(before * belongs.astype(jnp.float32), axis=0)
    return owner_of * SEGMENT + rank.astype(jnp.int32)


def sorted_targets(codes, per_owner):
    owners = codes.shape[0]
    cluster = jnp.where(codes < 0, -1, codes // SLOTS)
    slot = codes % SLOTS
    here = jnp.arange(per_owner, dtype=jnp.int32)
    one_hot = (cluster[:, :, None] == here[None, None, :]).astype(jnp.int32)
    count = jnp.sum(one_hot, axis=1)
    source = jnp.arange(owners, dtype=jnp.int32)
    before = jnp.sum(
        jnp.where((source[None, :] < source[:, None])[:, :, None], count[None, :, :], 0), axis=1
    )
    total = jnp.sum(count, axis=0)
    first = jnp.sum(jnp.where(here[None, :] < here[:, None], total[None, :], 0), axis=1)
    base = first[None, :] + before
    target = jnp.sum(one_hot * base[:, None, :], axis=2) + slot
    return jnp.where(codes < 0, -1, target), cluster, first


def shards(queries, keys, values, cluster_ids, slots, centroid_sums, centroid_counts, out_weight):
    owners = lax.axis_size("seq")
    row_width = queries.shape[1]
    per_owner = centroid_sums.shape[1]
    total = owners * SEGMENT
    cluster_of = cluster_ids[0]
    slot_of = slots[0]
    position = block_positions(cluster_of, owners, per_owner)
    code_of = cluster_of % per_owner * SLOTS + slot_of + 1
    codes = (
        jnp.sum(
            jnp.where(
                position[None, :] == jnp.arange(total, dtype=jnp.int32)[:, None],
                code_of[None, :],
                0,
            ),
            axis=1,
        )
        - 1
    )
    codes = lax.all_to_all(codes.reshape(owners, SEGMENT), "seq", 0, 0, tiled=True)
    packed = pack(position, queries, keys, values, total).reshape(owners, SEGMENT, 3 * row_width)
    rows = lax.all_to_all(packed, "seq", 0, 0, tiled=True).reshape(total, 3 * row_width)
    target, cluster, first = sorted_targets(codes, per_owner)
    first = jnp.pad(first, (0, 128 - per_owner)).reshape(1, 128)
    returned, centroids = attend_clusters(
        target, cluster, first, rows, centroid_sums[0], centroid_counts[0][:, None]
    )
    returned = lax.all_to_all(
        returned.reshape(owners, SEGMENT, row_width), "seq", 0, 0, tiled=True
    ).reshape(total, row_width)
    mixed = lax.psum_scatter(
        project(position, returned, out_weight), "head", scatter_dimension=0, tiled=True
    )
    return (mixed, centroids[None])


def solution(mesh):
    return jax.shard_map(
        shards,
        mesh=mesh,
        in_specs=(
            P("seq", "head"),
            P("seq", "head"),
            P("seq", "head"),
            P("head", "seq"),
            P("head", "seq"),
            P("head", "seq", None),
            P("head", "seq"),
            P("head", None),
        ),
        out_specs=(P(("seq", "head"), None), P("head", "seq", None)),
        check_vma=False,
    )
```

```python
import jax
import jax.numpy as jnp
from jax import lax
from jax.experimental import pallas as pl
from jax.experimental.pallas import tpu as pltpu
from jax.sharding import PartitionSpec as P

HD = 128
SLOTS = 3
SEGMENT = 48
TILE = 128
PACK_ROWS = 384
OUT_COLS = 512
HALVES = 2
NEG = -1e30

VMEM = pl.BlockSpec(memory_space=pltpu.VMEM)
BIG = pltpu.CompilerParams(vmem_limit_bytes=60 << 20)


def cost(flops, moved):
    return pl.CostEstimate(flops=flops, bytes_accessed=moved, transcendentals=0)


def pack_kernel(position_ref, values_ref, packed_ref):
    rows, tokens = packed_ref.shape[0], values_ref.shape[0]
    first = pl.program_id(0) * rows
    row_of = first + lax.broadcasted_iota(jnp.int32, (rows, tokens), 0)
    pick = (row_of == position_ref[...]).astype(jnp.bfloat16)
    packed_ref[...] = jnp.dot(
        pick, values_ref[...], preferred_element_type=jnp.float32
    ).astype(jnp.bfloat16)


def pack(position, values, rows):
    tokens, width = values.shape
    return pl.pallas_call(
        pack_kernel,
        grid=(rows // PACK_ROWS,),
        in_specs=[
            pl.BlockSpec((1, tokens), lambda i: (0, 0)),
            pl.BlockSpec((tokens, width), lambda i: (0, 0)),
        ],
        out_specs=pl.BlockSpec((PACK_ROWS, width), lambda i: (i, 0)),
        out_shape=jax.ShapeDtypeStruct((rows, width), jnp.bfloat16),
        cost_estimate=cost(2 * rows * tokens * width, 2 * width * (rows + tokens)),
    )(position.reshape(1, tokens), values)


def order_rows(target_ref, rows_ref, ordered_ref, offset):
    rows = rows_ref.shape[0]

    def order(step, carry):
        start = step * (2 * TILE)
        place = start + lax.broadcasted_iota(jnp.int32, (2 * TILE, rows), 0)
        pick = (place == target_ref[...]).astype(jnp.bfloat16)
        ordered_ref[pl.ds(start + offset, 2 * TILE), :] = jnp.dot(
            pick, rows_ref[...], preferred_element_type=jnp.float32
        ).astype(jnp.bfloat16)
        return carry

    lax.fori_loop(0, rows // (2 * TILE), order, 0)


def keys_kernel(target_ref, cluster_ref, rows_ref, sums_ref, counts_ref, ordered_ref, centroids_ref):
    rows, width = rows_ref.shape
    clusters = sums_ref.shape[0]
    belongs = lax.broadcasted_iota(jnp.int32, (clusters, rows), 0) == cluster_ref[...]
    batch_sums = jnp.dot(
        belongs.astype(jnp.bfloat16), rows_ref[...], preferred_element_type=jnp.float32
    )
    batch_counts = jnp.sum(belongs.astype(jnp.float32), axis=1, keepdims=True)
    centroids_ref[...] = (0.6 * sums_ref[...] + 0.4 * batch_sums) / (
        0.6 * counts_ref[...] + 0.4 * batch_counts
    )
    ordered_ref[0:TILE, :] = jnp.zeros((TILE, width), jnp.bfloat16)
    order_rows(target_ref, rows_ref, ordered_ref, TILE)


def order_keys(target, cluster, rows, sums, counts):
    total, width = rows.shape
    return pl.pallas_call(
        keys_kernel,
        in_specs=[VMEM] * 5,
        out_specs=[VMEM] * 2,
        out_shape=[
            jax.ShapeDtypeStruct((total + TILE, width), jnp.bfloat16),
            jax.ShapeDtypeStruct(sums.shape, jnp.float32),
        ],
        compiler_params=BIG,
        cost_estimate=cost(2 * total * total * width, 4 * total * width),
    )(target.reshape(1, total), cluster.reshape(1, total), rows, sums, counts)


def weights_kernel(target_ref, first_ref, keys_ref, rows_ref, weights_ref, ordered_ref):
    heads, rows = weights_ref.shape[:2]
    order_rows(target_ref, rows_ref, ordered_ref, 0)

    def score(step, carry):
        start = step * TILE
        place = start + lax.broadcasted_iota(jnp.int32, (TILE, first_ref.shape[1]), 0)
        first = first_ref[...]
        low = jnp.max(jnp.where(first <= place, first, 0), axis=1, keepdims=True)
        query_place = start + lax.broadcasted_iota(jnp.int32, (TILE, 2 * TILE), 0)
        key_place = start - TILE + lax.broadcasted_iota(jnp.int32, (TILE, 2 * TILE), 1)
        seen = (key_place <= query_place) & (key_place >= low)
        for head in range(heads):
            column = head * HD
            query = ordered_ref[pl.ds(start, TILE), column : column + HD]
            key = keys_ref[pl.ds(start, 2 * TILE), column : column + HD]
            scores = lax.dot_general(
                query, key, (((1,), (1,)), ((), ())), preferred_element_type=jnp.float32
            ) * (HD**-0.5)
            scores = jnp.where(seen, scores, NEG)
            shifted = jnp.exp(scores - jnp.max(scores, axis=1, keepdims=True))
            weights = shifted / jnp.sum(shifted, axis=1, keepdims=True)
            weights_ref[head, pl.ds(start, TILE), :] = weights.astype(jnp.bfloat16)
        return carry

    lax.fori_loop(0, rows // TILE, score, 0)


def attention_weights(target, first, keys, rows):
    total, width = rows.shape
    heads = width // HD
    return pl.pallas_call(
        weights_kernel,
        in_specs=[VMEM] * 4,
        out_specs=VMEM,
        out_shape=jax.ShapeDtypeStruct((heads, total, 2 * TILE), jnp.bfloat16),
        scratch_shapes=[pltpu.VMEM((total, width), jnp.bfloat16)],
        compiler_params=BIG,
        cost_estimate=cost(4 * total * total * width, 8 * total * width),
    )(target.reshape(1, total), first, keys, rows)


def attend_kernel(
    row_target_ref, column_target_ref, weights_ref, rows_ref, returned_ref, ordered_ref, attended_ref
):
    rows, width = rows_ref.shape
    ordered_ref[0:TILE, :] = jnp.zeros((TILE, width), jnp.bfloat16)
    order_rows(row_target_ref, rows_ref, ordered_ref, TILE)

    def attend(step, carry):
        start = step * TILE
        for head in range(width // HD):
            column = head * HD
            value = ordered_ref[pl.ds(start, 2 * TILE), column : column + HD]
            attended_ref[pl.ds(start, TILE), column : column + HD] = jnp.dot(
                weights_ref[head, pl.ds(start, TILE), :],
                value,
                preferred_element_type=jnp.float32,
            ).astype(jnp.bfloat16)
        return carry

    lax.fori_loop(0, rows // TILE, attend, 0)

    def restore(step, carry):
        start = step * (2 * TILE)
        target = column_target_ref[pl.ds(start, 2 * TILE), :]
        pick = (lax.broadcasted_iota(jnp.int32, (2 * TILE, rows), 1) == target).astype(jnp.bfloat16)
        returned_ref[pl.ds(start, 2 * TILE), :] = jnp.dot(
            pick, attended_ref[...], preferred_element_type=jnp.float32
        ).astype(jnp.bfloat16)
        return carry

    lax.fori_loop(0, rows // (2 * TILE), restore, 0)


def attend_half(half, target, weights, rows):
    total, width = rows.shape
    heads, part = weights.shape[0] // HALVES, width // HALVES
    return pl.pallas_call(
        attend_kernel,
        grid=(1,),
        in_specs=[
            pl.BlockSpec((1, total), lambda i: (0, 0)),
            pl.BlockSpec((total, 1), lambda i: (0, 0)),
            pl.BlockSpec((heads, total, 2 * TILE), lambda i: (half, 0, 0)),
            pl.BlockSpec((total, part), lambda i: (0, half)),
        ],
        out_specs=pl.BlockSpec((total, part), lambda i: (0, 0)),
        out_shape=jax.ShapeDtypeStruct((total, part), jnp.bfloat16),
        scratch_shapes=[
            pltpu.VMEM((total + TILE, part), jnp.bfloat16),
            pltpu.VMEM((total, part), jnp.bfloat16),
        ],
        compiler_params=BIG,
        cost_estimate=cost(4 * total * total * part, 8 * total * part),
    )(target.reshape(1, total), target.reshape(total, 1), weights, rows)


def unpack_kernel(position_ref, rows_ref, *out_refs):
    quarter, total = out_refs[0].shape[0], rows_ref.shape[0]
    for index, out_ref in enumerate(out_refs):
        position = position_ref[index * quarter : (index + 1) * quarter, :]
        pick = (lax.broadcasted_iota(jnp.int32, (quarter, total), 1) == position).astype(
            jnp.bfloat16
        )
        out_ref[...] = jnp.dot(pick, rows_ref[...], preferred_element_type=jnp.float32).astype(
            jnp.bfloat16
        )


def unpack(position, rows, parts):
    tokens = position.shape[0]
    total, width = rows.shape
    return pl.pallas_call(
        unpack_kernel,
        in_specs=[VMEM] * 2,
        out_specs=[VMEM] * parts,
        out_shape=[jax.ShapeDtypeStruct((tokens // parts, width), jnp.bfloat16)] * parts,
        cost_estimate=cost(2 * tokens * total * width, 2 * width * (total + tokens)),
    )(position.reshape(tokens, 1), rows)


def project_kernel(core_ref, *refs):
    groups = (len(refs) - 1) // (HALVES + 2)
    row_refs = refs[: groups * HALVES]
    own_ref = refs[groups * HALVES]
    weight_refs = refs[groups * HALVES + 1 : -2]
    out_ref, rows_ref = refs[-2:]
    part = row_refs[0].shape[1]
    width = part * HALVES
    step = pl.program_id(0)

    @pl.when(step == 0)
    def _():
        for index, ref in enumerate(row_refs):
            rows_ref[:, index * part : (index + 1) * part] = ref[...]

    def product(side):
        total = jnp.dot(rows_ref[:, :width], own_ref[...], preferred_element_type=jnp.float32)
        for index, ref in enumerate(weight_refs[side * (groups - 1) : (side + 1) * (groups - 1)]):
            total += jnp.dot(
                rows_ref[:, (index + 1) * width : (index + 2) * width],
                ref[...],
                preferred_element_type=jnp.float32,
            )
        out_ref[...] = total.astype(jnp.bfloat16)

    steps = pl.num_programs(0)

    @pl.when(step < steps // 2)
    def _():
        product(0)

    @pl.when(step >= steps // 2)
    def _():
        product(1)


def project(core, rows, own, near, far):
    tokens, part = rows[0].shape
    width, columns = own.shape
    groups = len(near) + 1
    steps = columns // OUT_COLS
    middle = steps // 2
    placed = lambda i, core: (0, lax.rem(core[0] * middle + i, steps))
    return pl.pallas_call(
        project_kernel,
        grid_spec=pltpu.PrefetchScalarGridSpec(
            num_scalar_prefetch=1,
            grid=(steps,),
            in_specs=[pl.BlockSpec((tokens, part), lambda i, core: (0, 0))] * len(rows)
            + [pl.BlockSpec((width, OUT_COLS), placed)]
            + [pl.BlockSpec((width, OUT_COLS), lambda i, core: (0, jnp.minimum(i, middle - 1)))]
            * len(near)
            + [pl.BlockSpec((width, OUT_COLS), lambda i, core: (0, jnp.maximum(i - middle, 0)))]
            * len(far),
            out_specs=pl.BlockSpec((tokens, OUT_COLS), placed),
            scratch_shapes=[pltpu.VMEM((tokens, groups * width), jnp.bfloat16)],
        ),
        out_shape=jax.ShapeDtypeStruct((tokens, columns), jnp.bfloat16),
        compiler_params=BIG,
        cost_estimate=cost(2 * tokens * groups * width * columns, 2 * groups * width * columns),
    )(core, *rows, own, *near, *far)


def block_positions(cluster_of, owners, per_owner):
    tokens = cluster_of.shape[0]
    owner_of = cluster_of // per_owner
    belongs = (jnp.arange(owners, dtype=jnp.int32)[:, None] == owner_of[None, :]).astype(
        jnp.bfloat16
    )
    token = jnp.arange(tokens, dtype=jnp.int32)
    earlier = (token[:, None] < token[None, :]).astype(jnp.bfloat16)
    before = jnp.dot(belongs, earlier, preferred_element_type=jnp.float32)
    rank = jnp.sum(before * belongs.astype(jnp.float32), axis=0)
    return owner_of * SEGMENT + rank.astype(jnp.int32)


def sorted_targets(codes, per_owner):
    owners = codes.shape[0]
    cluster = jnp.where(codes < 0, -1, codes // SLOTS)
    slot = codes % SLOTS
    here = jnp.arange(per_owner, dtype=jnp.int32)
    one_hot = (cluster[:, :, None] == here[None, None, :]).astype(jnp.int32)
    count = jnp.sum(one_hot, axis=1)
    source = jnp.arange(owners, dtype=jnp.int32)
    before = jnp.sum(
        jnp.where((source[None, :] < source[:, None])[:, :, None], count[None, :, :], 0), axis=1
    )
    total = jnp.sum(count, axis=0)
    first = jnp.sum(jnp.where(here[None, :] < here[:, None], total[None, :], 0), axis=1)
    base = first[None, :] + before
    target = jnp.sum(one_hot * base[:, None, :], axis=2) + slot
    return jnp.where(codes < 0, -1, target), cluster, first


def exchange(rows, owners):
    width = rows.shape[1]
    rows = lax.all_to_all(rows.reshape(owners, SEGMENT, width), "seq", 0, 0, tiled=True)
    return rows.reshape(owners * SEGMENT, width)


def shards(queries, keys, values, cluster_ids, slots, centroid_sums, centroid_counts, out_weight):
    owners = lax.axis_size("seq")
    groups = lax.axis_size("head")
    tokens = queries.shape[0]
    columns = out_weight.shape[1]
    per_owner = centroid_sums.shape[1]
    total = owners * SEGMENT
    cluster_of = cluster_ids[0]
    slot_of = slots[0]
    core = lax.axis_index("seq") % 2
    group = lax.axis_index("head")

    def shift(value, by):
        return lax.ppermute(value, "head", [(i, (i + by) % groups) for i in range(groups)])

    def swap(value):
        return lax.ppermute(value, "seq", [(i, i ^ 1) for i in range(owners)])

    position = block_positions(cluster_of, owners, per_owner)
    packed_keys = pack(position, keys, total)
    rows_keys = exchange(packed_keys, owners)

    position_later, _ = lax.optimization_barrier((position, packed_keys))
    half_weight = lax.dynamic_slice_in_dim(out_weight, core * (columns // 2), columns // 2, 1)
    near = [shift(half_weight, by) for by in range(1, groups)]
    far = [swap(value) for value in near]

    code_of = cluster_of % per_owner * SLOTS + slot_of + 1
    codes = (
        jnp.sum(
            jnp.where(
                position_later[None, :] == jnp.arange(total, dtype=jnp.int32)[:, None],
                code_of[None, :],
                0,
            ),
            axis=1,
        )
        - 1
    )
    codes = lax.all_to_all(codes.reshape(owners, SEGMENT), "seq", 0, 0, tiled=True)
    rows_queries = exchange(pack(position_later, queries, total), owners)
    rows_values = exchange(pack(position_later, values, total), owners)

    target, cluster, first = sorted_targets(codes, per_owner)
    first = jnp.pad(first, (0, 128 - per_owner)).reshape(1, 128)
    ordered_keys, centroids = order_keys(
        target, cluster, rows_keys, centroid_sums[0], centroid_counts[0][:, None]
    )
    weights = attention_weights(target, first, ordered_keys, rows_queries)

    quarter = jnp.arange(groups, dtype=jnp.int32)
    rolled = position.reshape(groups, tokens // groups)[(group + quarter) % groups].reshape(tokens)
    halves = []
    for half in range(HALVES):
        returned = exchange(attend_half(half, target, weights, rows_values), owners)
        pieces = unpack(rolled, returned, groups)
        halves.append([pieces[0]] + [shift(pieces[by], by) for by in range(1, groups)])
    rows = [halves[half][by] for by in range(groups) for half in range(HALVES)]
    mixed = project(core.reshape(1), rows, out_weight, near, far)
    return (mixed, centroids[None])


def solution(mesh):
    return jax.shard_map(
        shards,
        mesh=mesh,
        in_specs=(
            P("seq", "head"),
            P("seq", "head"),
            P("seq", "head"),
            P("head", "seq"),
            P("head", "seq"),
            P("head", "seq", None),
            P("head", "seq"),
            P("head", None),
        ),
        out_specs=(P(("seq", "head"), None), P("head", "seq", None)),
        check_vma=False,
    )
```

```python
import jax
import jax.numpy as jnp
from jax import lax
from jax.experimental import pallas as pl
from jax.experimental.pallas import tpu as pltpu
from jax.sharding import PartitionSpec as P

HD = 128
SLOTS = 3
SEGMENT = 48
TILE = 128
PACK_ROWS = 384
OUT_COLS = 512
HALVES = 2
NEG = -1e30
LANES = 128

VMEM = pl.BlockSpec(memory_space=pltpu.VMEM)
BIG = pltpu.CompilerParams(vmem_limit_bytes=60 << 20)


def cost(flops, moved):
    return pl.CostEstimate(flops=flops, bytes_accessed=moved, transcendentals=0)


def pack_kernel(position_ref, values_ref, packed_ref):
    rows, tokens = packed_ref.shape[0], values_ref.shape[0]
    first = pl.program_id(0) * rows
    row_of = first + lax.broadcasted_iota(jnp.int32, (rows, tokens), 0)
    pick = (row_of == position_ref[...]).astype(jnp.bfloat16)
    packed_ref[...] = jnp.dot(
        pick, values_ref[...], preferred_element_type=jnp.float32
    ).astype(jnp.bfloat16)


def pack(position, values, rows):
    tokens, width = values.shape
    return pl.pallas_call(
        pack_kernel,
        grid=(rows // PACK_ROWS,),
        in_specs=[
            pl.BlockSpec((1, tokens), lambda i: (0, 0)),
            pl.BlockSpec((tokens, width), lambda i: (0, 0)),
        ],
        out_specs=pl.BlockSpec((PACK_ROWS, width), lambda i: (i, 0)),
        out_shape=jax.ShapeDtypeStruct((rows, width), jnp.bfloat16),
        cost_estimate=cost(2 * rows * tokens * width, 2 * width * (rows + tokens)),
    )(position.reshape(1, tokens), values)


def pack_coded_kernel(position_ref, values_ref, codes_ref, packed_ref):
    rows, tokens = packed_ref.shape[0], values_ref.shape[0]
    width = values_ref.shape[1]
    first = pl.program_id(0) * rows
    row_of = first + lax.broadcasted_iota(jnp.int32, (rows, tokens), 0)
    pick = (row_of == position_ref[...]).astype(jnp.bfloat16)
    for ref, low in ((values_ref, 0), (codes_ref, width)):
        packed_ref[:, low : low + ref.shape[1]] = jnp.dot(
            pick, ref[...], preferred_element_type=jnp.float32
        ).astype(jnp.bfloat16)


def pack_coded(position, values, codes, rows):
    tokens, width = values.shape
    codes = jnp.broadcast_to(codes.astype(jnp.bfloat16)[:, None], (tokens, LANES))
    return pl.pallas_call(
        pack_coded_kernel,
        grid=(rows // PACK_ROWS,),
        in_specs=[
            pl.BlockSpec((1, tokens), lambda i: (0, 0)),
            pl.BlockSpec((tokens, width), lambda i: (0, 0)),
            pl.BlockSpec((tokens, LANES), lambda i: (0, 0)),
        ],
        out_specs=pl.BlockSpec((PACK_ROWS, width + LANES), lambda i: (i, 0)),
        out_shape=jax.ShapeDtypeStruct((rows, width + LANES), jnp.bfloat16),
        cost_estimate=cost(2 * rows * tokens * width, 2 * width * (rows + tokens)),
    )(position.reshape(1, tokens), values, codes)


def order_rows(target_ref, rows_ref, ordered_ref, offset):
    rows, width = rows_ref.shape[0], ordered_ref.shape[1]

    def order(step, carry):
        start = step * (2 * TILE)
        place = start + lax.broadcasted_iota(jnp.int32, (2 * TILE, rows), 0)
        pick = (place == target_ref[...]).astype(jnp.bfloat16)
        ordered_ref[pl.ds(start + offset, 2 * TILE), :] = jnp.dot(
            pick, rows_ref[:, :width], preferred_element_type=jnp.float32
        ).astype(jnp.bfloat16)
        return carry

    lax.fori_loop(0, rows // (2 * TILE), order, 0)


def keys_kernel(target_ref, cluster_ref, rows_ref, sums_ref, counts_ref, ordered_ref, centroids_ref):
    rows, width = rows_ref.shape[0], ordered_ref.shape[1]
    clusters = sums_ref.shape[0]
    belongs = lax.broadcasted_iota(jnp.int32, (clusters, rows), 0) == cluster_ref[...]
    batch_sums = jnp.dot(
        belongs.astype(jnp.bfloat16), rows_ref[:, :width], preferred_element_type=jnp.float32
    )
    batch_counts = jnp.sum(belongs.astype(jnp.float32), axis=1, keepdims=True)
    centroids_ref[...] = (0.6 * sums_ref[...] + 0.4 * batch_sums) / (
        0.6 * counts_ref[...] + 0.4 * batch_counts
    )
    ordered_ref[0:TILE, :] = jnp.zeros((TILE, width), jnp.bfloat16)
    order_rows(target_ref, rows_ref, ordered_ref, TILE)


def order_keys(target, cluster, rows, sums, counts):
    total, width = rows.shape[0], sums.shape[1]
    return pl.pallas_call(
        keys_kernel,
        in_specs=[VMEM] * 5,
        out_specs=[VMEM] * 2,
        out_shape=[
            jax.ShapeDtypeStruct((total + TILE, width), jnp.bfloat16),
            jax.ShapeDtypeStruct(sums.shape, jnp.float32),
        ],
        compiler_params=BIG,
        cost_estimate=cost(2 * total * total * width, 4 * total * width),
    )(target.reshape(1, total), cluster.reshape(1, total), rows, sums, counts)


def weights_kernel(target_ref, first_ref, keys_ref, rows_ref, weights_ref, ordered_ref):
    heads, rows = weights_ref.shape[:2]
    order_rows(target_ref, rows_ref, ordered_ref, 0)

    def score(step, carry):
        start = step * TILE
        place = start + lax.broadcasted_iota(jnp.int32, (TILE, first_ref.shape[1]), 0)
        first = first_ref[...]
        low = jnp.max(jnp.where(first <= place, first, 0), axis=1, keepdims=True)
        query_place = start + lax.broadcasted_iota(jnp.int32, (TILE, 2 * TILE), 0)
        key_place = start - TILE + lax.broadcasted_iota(jnp.int32, (TILE, 2 * TILE), 1)
        seen = (key_place <= query_place) & (key_place >= low)
        for head in range(heads):
            column = head * HD
            query = ordered_ref[pl.ds(start, TILE), column : column + HD]
            key = keys_ref[pl.ds(start, 2 * TILE), column : column + HD]
            scores = lax.dot_general(
                query, key, (((1,), (1,)), ((), ())), preferred_element_type=jnp.float32
            ) * (HD**-0.5)
            scores = jnp.where(seen, scores, NEG)
            shifted = jnp.exp(scores - jnp.max(scores, axis=1, keepdims=True))
            weights = shifted / jnp.sum(shifted, axis=1, keepdims=True)
            weights_ref[head, pl.ds(start, TILE), :] = weights.astype(jnp.bfloat16)
        return carry

    lax.fori_loop(0, rows // TILE, score, 0)


def attention_weights(target, first, keys, rows):
    total, width = rows.shape
    heads = width // HD
    return pl.pallas_call(
        weights_kernel,
        in_specs=[VMEM] * 4,
        out_specs=VMEM,
        out_shape=jax.ShapeDtypeStruct((heads, total, 2 * TILE), jnp.bfloat16),
        scratch_shapes=[pltpu.VMEM((total, width), jnp.bfloat16)],
        compiler_params=BIG,
        cost_estimate=cost(4 * total * total * width, 8 * total * width),
    )(target.reshape(1, total), first, keys, rows)


def attend_kernel(
    row_target_ref, column_target_ref, weights_ref, rows_ref, returned_ref, ordered_ref, attended_ref
):
    rows, width = rows_ref.shape
    ordered_ref[0:TILE, :] = jnp.zeros((TILE, width), jnp.bfloat16)
    order_rows(row_target_ref, rows_ref, ordered_ref, TILE)

    def attend(step, carry):
        start = step * TILE
        for head in range(width // HD):
            column = head * HD
            value = ordered_ref[pl.ds(start, 2 * TILE), column : column + HD]
            attended_ref[pl.ds(start, TILE), column : column + HD] = jnp.dot(
                weights_ref[head, pl.ds(start, TILE), :],
                value,
                preferred_element_type=jnp.float32,
            ).astype(jnp.bfloat16)
        return carry

    lax.fori_loop(0, rows // TILE, attend, 0)

    def restore(step, carry):
        start = step * (2 * TILE)
        target = column_target_ref[pl.ds(start, 2 * TILE), :]
        pick = (lax.broadcasted_iota(jnp.int32, (2 * TILE, rows), 1) == target).astype(jnp.bfloat16)
        returned_ref[pl.ds(start, 2 * TILE), :] = jnp.dot(
            pick, attended_ref[...], preferred_element_type=jnp.float32
        ).astype(jnp.bfloat16)
        return carry

    lax.fori_loop(0, rows // (2 * TILE), restore, 0)


def attend_half(half, target, weights, rows):
    total, width = rows.shape
    heads, part = weights.shape[0] // HALVES, width // HALVES
    return pl.pallas_call(
        attend_kernel,
        grid=(1,),
        in_specs=[
            pl.BlockSpec((1, total), lambda i: (0, 0)),
            pl.BlockSpec((total, 1), lambda i: (0, 0)),
            pl.BlockSpec((heads, total, 2 * TILE), lambda i: (half, 0, 0)),
            pl.BlockSpec((total, part), lambda i: (0, half)),
        ],
        out_specs=pl.BlockSpec((total, part), lambda i: (0, 0)),
        out_shape=jax.ShapeDtypeStruct((total, part), jnp.bfloat16),
        scratch_shapes=[
            pltpu.VMEM((total + TILE, part), jnp.bfloat16),
            pltpu.VMEM((total, part), jnp.bfloat16),
        ],
        compiler_params=BIG,
        cost_estimate=cost(4 * total * total * part, 8 * total * part),
    )(target.reshape(1, total), target.reshape(total, 1), weights, rows)


def unpack_kernel(position_ref, rows_ref, *out_refs):
    quarter, total = out_refs[0].shape[0], rows_ref.shape[0]
    for index, out_ref in enumerate(out_refs):
        position = position_ref[index * quarter : (index + 1) * quarter, :]
        pick = (lax.broadcasted_iota(jnp.int32, (quarter, total), 1) == position).astype(
            jnp.bfloat16
        )
        out_ref[...] = jnp.dot(pick, rows_ref[...], preferred_element_type=jnp.float32).astype(
            jnp.bfloat16
        )


def unpack(position, rows, parts):
    tokens = position.shape[0]
    total, width = rows.shape
    return pl.pallas_call(
        unpack_kernel,
        in_specs=[VMEM] * 2,
        out_specs=[VMEM] * parts,
        out_shape=[jax.ShapeDtypeStruct((tokens // parts, width), jnp.bfloat16)] * parts,
        cost_estimate=cost(2 * tokens * total * width, 2 * width * (total + tokens)),
    )(position.reshape(tokens, 1), rows)


def project_kernel(core_ref, *refs):
    row_refs, weight_refs, out_ref, rows_ref = refs[:8], refs[8:13], refs[13], refs[14]
    part = row_refs[0].shape[1]
    step = pl.program_id(0)

    for core, pieces in ((0, (0, 1, 2, 3, 6, 7, 4, 5)), (1, (0, 1, 6, 7, 2, 3, 5, 4))):

        @pl.when((step == 0) & (core_ref[0] == core))
        def _():
            for index, piece in enumerate(pieces):
                rows_ref[:, index * part : (index + 1) * part] = row_refs[piece][...]

    total, low = None, 0
    for ref in weight_refs:
        depth = ref.shape[0]
        term = jnp.dot(
            rows_ref[:, low : low + depth], ref[...], preferred_element_type=jnp.float32
        )
        total, low = term if total is None else total + term, low + depth
    out_ref[...] = total.astype(jnp.bfloat16)


def project(core, rows, weights):
    tokens, part = rows[0].shape
    columns = weights[0].shape[1]
    depth = sum(value.shape[0] for value in weights)
    return pl.pallas_call(
        project_kernel,
        grid_spec=pltpu.PrefetchScalarGridSpec(
            num_scalar_prefetch=1,
            grid=(columns // OUT_COLS,),
            in_specs=[pl.BlockSpec((tokens, part), lambda i, core: (0, 0))] * len(rows)
            + [
                pl.BlockSpec((value.shape[0], OUT_COLS), lambda i, core: (0, i))
                for value in weights
            ],
            out_specs=pl.BlockSpec((tokens, OUT_COLS), lambda i, core: (0, i)),
            scratch_shapes=[pltpu.VMEM((tokens, depth), jnp.bfloat16)],
        ),
        out_shape=jax.ShapeDtypeStruct((tokens, columns), jnp.bfloat16),
        compiler_params=BIG,
        cost_estimate=cost(2 * tokens * depth * columns, 2 * depth * columns),
    )(core, *rows, *weights)


def block_positions(cluster_of, owners, per_owner):
    tokens = cluster_of.shape[0]
    owner_of = cluster_of // per_owner
    belongs = (jnp.arange(owners, dtype=jnp.int32)[:, None] == owner_of[None, :]).astype(
        jnp.bfloat16
    )
    token = jnp.arange(tokens, dtype=jnp.int32)
    earlier = (token[:, None] < token[None, :]).astype(jnp.bfloat16)
    before = jnp.dot(belongs, earlier, preferred_element_type=jnp.float32)
    rank = jnp.sum(before * belongs.astype(jnp.float32), axis=0)
    return owner_of * SEGMENT + rank.astype(jnp.int32)


def sorted_targets(codes, per_owner):
    owners = codes.shape[0]
    cluster = jnp.where(codes < 0, -1, codes // SLOTS)
    slot = codes % SLOTS
    here = jnp.arange(per_owner, dtype=jnp.int32)
    one_hot = (cluster[:, :, None] == here[None, None, :]).astype(jnp.int32)
    count = jnp.sum(one_hot, axis=1)
    source = jnp.arange(owners, dtype=jnp.int32)
    before = jnp.sum(
        jnp.where((source[None, :] < source[:, None])[:, :, None], count[None, :, :], 0), axis=1
    )
    total = jnp.sum(count, axis=0)
    first = jnp.sum(jnp.where(here[None, :] < here[:, None], total[None, :], 0), axis=1)
    base = first[None, :] + before
    target = jnp.sum(one_hot * base[:, None, :], axis=2) + slot
    return jnp.where(codes < 0, -1, target), cluster, first


def exchange(rows, owners):
    width = rows.shape[1]
    rows = lax.all_to_all(rows.reshape(owners, SEGMENT, width), "seq", 0, 0, tiled=True)
    return rows.reshape(owners * SEGMENT, width)


def shards(queries, keys, values, cluster_ids, slots, centroid_sums, centroid_counts, out_weight):
    owners = lax.axis_size("seq")
    groups = lax.axis_size("head")
    tokens = queries.shape[0]
    per_owner = centroid_sums.shape[1]
    total = owners * SEGMENT
    cluster_of = cluster_ids[0]
    slot_of = slots[0]
    core = lax.axis_index("seq") % 2
    group = lax.axis_index("head")

    def shift(value, by):
        return lax.ppermute(value, "head", [(i, (i + by) % groups) for i in range(groups)])

    def swap(value):
        return lax.ppermute(value, "seq", [(i, i ^ 1) for i in range(owners)])

    def spread(value):
        pairs = [
            (seq * groups + i, seq * groups + (i + 1 - 2 * (seq % 2)) % groups)
            for seq in range(owners)
            for i in range(groups)
        ]
        return lax.ppermute(value, ("seq", "head"), pairs)

    def after(value, *others):
        return lax.optimization_barrier((value, *others))[0]

    near = spread(out_weight)
    position = block_positions(cluster_of, owners, per_owner)
    code_of = cluster_of % per_owner * SLOTS + slot_of + 1
    packed_keys = pack_coded(position, keys, code_of, total)
    rows_keys = exchange(packed_keys, owners)
    position_later = after(position, packed_keys)
    packed_queries = pack(position_later, queries, total)
    rows_queries = exchange(after(packed_queries, rows_keys), owners)
    packed_values = pack(after(position_later, packed_queries), values, total)
    rows_values = exchange(after(packed_values, rows_queries), owners)

    codes = rows_keys[:, keys.shape[1]].astype(jnp.int32).reshape(owners, SEGMENT) - 1
    target, cluster, first = sorted_targets(codes, per_owner)
    first = jnp.pad(first, (0, LANES - per_owner)).reshape(1, LANES)
    ordered_keys, centroids = order_keys(
        target, cluster, rows_keys, centroid_sums[0], centroid_counts[0][:, None]
    )
    weights = attention_weights(target, first, ordered_keys, rows_queries)

    near = after(near, rows_queries)
    far = swap(near)
    depth = out_weight.shape[0] // 2
    opposite = [spread(lax.dynamic_slice_in_dim(near, core * depth, depth, 0))]

    quarter = jnp.arange(groups, dtype=jnp.int32)
    rolled = position.reshape(groups, tokens // groups)[(group + quarter) % groups].reshape(tokens)
    halves = []
    for half in range(HALVES):
        attended = attend_half(half, target if half == 0 else after(target, attended), weights, rows_values)
        if half == 0:
            opposite.append(swap(after(opposite[0], attended)))
            returned = exchange(attended, owners)
        else:
            returned = exchange(after(attended, returned), owners)
        pieces = unpack(rolled, returned, groups)
        halves.append([pieces[0]] + [shift(pieces[by], by) for by in range(1, groups)])
    rows = [halves[half][by] for by in range(groups) for half in range(HALVES)]
    mixed = project(core.reshape(1), rows, [out_weight, near, far, *opposite])
    return (mixed, centroids[None])


def solution(mesh):
    return jax.shard_map(
        shards,
        mesh=mesh,
        in_specs=(
            P("seq", "head"),
            P("seq", "head"),
            P("seq", "head"),
            P("head", "seq"),
            P("head", "seq"),
            P("head", "seq", None),
            P("head", "seq"),
            P("head", None),
        ),
        out_specs=(P(("seq", "head"), None), P("head", "seq", None)),
        check_vma=False,
    )
```
